32 devices in a mesh: row: 4 (over x, core), col: 8 (over z, y).
Axes of the slice: x: 2, y: 2, z: 4, core: 2. Of those that a mesh axis runs over, the one named last changes fastest.
Arguments:
- matrix: float32 [24576, 24576], P('row', 'col'), may hold values from -6 to 6
Outputs:
- y_block: float32 [4, 24576], P(None, 'row')
- reflectors: float32 [4, 24576], P(None, 'row')
- t_factor: float32 [4, 4], replicated
The draws below stay inside these ranges and needn't reach their ends.
All inputs are finite; a program needn't handle non-finite values.
Results may differ from the reference program's by a relative error of at most 0.0003.
Values sent between devices are 32-bit elements; how exact they have to be, the bound alone decides.
A program may use at most 128 MiB of HBM per device.

```python
import jax
import jax.numpy as jnp
from jax import lax

N = 24576
K = 4


def steps_of(rng, shape, split, smallest, top_value):
    level = 1.0
    for dim, shards_of in split:
        heights = jax.random.uniform(jax.random.fold_in(jax.random.fold_in(rng, 6), dim), (shards_of,), jnp.float32, smallest / len(split), top_value / len(split))
        level = level * jnp.repeat(jnp.exp(heights), shape[dim] // shards_of).reshape((-1,) + (1,) * (len(shape) - 1 - dim))
    return level


def normal_values(key, shape, scale, bound, shards=(), held_as=jnp.bfloat16):
    gain = steps_of(key, shape, shards, -0.22, 0.18) if shards else 1.0
    values = jax.random.normal(key, shape, jnp.float32) * scale * gain
    return jnp.minimum(jnp.maximum(values, -bound), bound).astype(held_as)


def setup_inputs(seed: int = 0) -> dict:
    key_list = jax.random.split(jax.random.key(seed), 2)
    matrix = normal_values(key_list[0], (N, N), 1.0, 6.0, ((0, 4), (1, 8)), jnp.float32)
    return dict(matrix=matrix)


precise = lax.Precision.HIGHEST

def householder(pivot_value, squares):
    length = jnp.sqrt(pivot_value * pivot_value + squares)
    signed = jnp.where(pivot_value >= 0, 1.0, -1.0)
    diagonal = -signed * length
    factor = (diagonal - pivot_value) / diagonal
    return (factor, pivot_value - diagonal)

def finish(product, cross_dots, y_rows, t_block, factor, panel_step):
    new_column = factor * (product - jnp.dot(cross_dots, y_rows, precision=precise))
    t_column = -factor * jnp.dot(t_block, cross_dots, precision=precise)
    slots = jnp.arange(K, dtype=jnp.int32)
    t_column = jnp.where(slots == panel_step, factor, t_column)
    t_block = jnp.where(slots[None, :] == panel_step, t_column[:, None], t_block)
    y_rows = jnp.where(slots[:, None] == panel_step, new_column[None, :], y_rows)
    return (y_rows, t_block)

def reference(matrix):
    extent = matrix.shape[0]
    all_rows = jnp.arange(extent, dtype=jnp.int32)
    slots = jnp.arange(K, dtype=jnp.int32)

    def advance(panel_step, carried):
        y_rows, v_rows, t_block = carried
        column = lax.dynamic_index_in_dim(matrix, panel_step, 1, keepdims=False)
        v_entry = lax.dynamic_index_in_dim(v_rows, panel_step, 1, keepdims=False)
        column = column - jnp.dot(v_entry, y_rows, precision=precise)
        left_dots = jnp.dot(v_rows, column, precision=precise)
        column = column - jnp.dot(jnp.dot(t_block.T, left_dots, precision=precise), v_rows, precision=precise)
        below = all_rows > panel_step + 1
        squares = jnp.sum(jnp.where(below, column * column, 0.0))
        pivot_value = lax.dynamic_index_in_dim(column, panel_step + 1, 0, keepdims=False)
        factor, divisor = householder(pivot_value, squares)
        reflect = jnp.where(below, column / divisor, 0.0) + (all_rows == panel_step + 1).astype(column.dtype)
        product = jnp.dot(matrix, reflect, precision=precise)
        cross_dots = jnp.dot(v_rows, reflect, precision=precise)
        y_rows, t_block = finish(product, cross_dots, y_rows, t_block, factor, panel_step)
        v_rows = jnp.where(slots[:, None] == panel_step, reflect[None, :], v_rows)
        return (y_rows, v_rows, t_block)
    start = (jnp.zeros((K, extent), jnp.float32), jnp.zeros((K, extent), jnp.float32), jnp.zeros((K, K), jnp.float32))
    y_rows, v_rows, t_block = lax.fori_loop(0, K, advance, start)
    return (y_rows, v_rows, t_block)
```

```python
import functools

import jax
import jax.numpy as jnp
from jax import lax
from jax.experimental import pallas as pl
from jax.experimental.pallas import tpu as pltpu
from jax.sharding import PartitionSpec as P

K = 4
LANES = 128
MESH = pl.DeviceIdType.MESH
VMEM_BYTES = 67043328
SPARE_BYTES = 5 * 2**19


def plan(R, C, rows, cols):
    q = C // R
    m = cols // LANES
    G = 8 if m % 8 == 0 else m
    ng = m // G
    groups = q * ng
    ring = max(4, q)
    room = (VMEM_BYTES - SPARE_BYTES) // (LANES * cols * 4)
    sp = 0
    while (G - sp) * groups + ring > room:
        sp += 1
    return q, m, G, ng, groups, ring, sp


def lane_total(row):
    return jnp.sum(row, axis=-1, keepdims=True)


def kernel(
    R, C, a_hbm, y_ref, v_ref, t_ref,
    res, ring, acc, pan, av, xs, pbuf, rbuf, sbuf, rnd, vy, ob, vs, ys, ps,
    res_sem, ring_sem, pan_sem, pan_send, av_sem, p_send, p_recv, s_send, s_recv, o_send, o_recv,
):
    rows, cols = a_hbm.shape
    q, m, G, ng, groups, nring, sp = plan(R, C, rows, cols)
    rp = G - sp
    r = lax.axis_index("row")
    c = lax.axis_index("col")

    def send(src, dst, send_sem, recv_sem, tr, tc):
        same = jnp.logical_and(tr == r, tc == c)

        @pl.when(jnp.logical_not(same))
        def _():
            pltpu.make_async_remote_copy(
                src, dst, send_sem, recv_sem, device_id=(tr, tc), device_id_type=MESH
            ).start()

        @pl.when(same)
        def _():
            pltpu.make_async_copy(src, dst, recv_sem).start()

    def sent(src, dst, send_sem, recv_sem, tr, tc):
        same = jnp.logical_and(tr == r, tc == c)

        @pl.when(jnp.logical_not(same))
        def _():
            pltpu.make_async_remote_copy(
                src, dst, send_sem, recv_sem, device_id=(tr, tc), device_id_type=MESH
            ).wait_send()

    def arrived(ref, sem):
        pltpu.make_async_copy(ref, ref, sem).wait()

    def panel_copy(t):
        return pltpu.make_async_copy(
            a_hbm.at[pl.ds(pl.multiple_of(t * LANES, LANES), LANES), pl.ds(0, LANES)],
            ring.at[lax.div(t, m), :, pl.ds(pl.multiple_of(lax.rem(t, m) * LANES, LANES), LANES)],
            pan_sem,
        )

    @pl.when(c == 0)
    def _():
        @pl.loop(0, q * m)
        def _(t):
            panel_copy(t).start()

    def res_copy(g, i):
        row = pl.multiple_of((g * G + i) * LANES, LANES)
        k = g * rp + i
        return pltpu.make_async_copy(a_hbm.at[pl.ds(row, LANES)], res.at[k], res_sem.at[k])

    def ring_copy(seq):
        n = lax.rem(seq, groups * sp)
        g, u = lax.div(n, sp), lax.rem(n, sp)
        row = pl.multiple_of((g * G + rp + u) * LANES, LANES)
        slot = lax.rem(seq, nring)
        return pltpu.make_async_copy(a_hbm.at[pl.ds(row, LANES)], ring.at[slot], ring_sem.at[slot])

    @pl.loop(0, groups)
    def _(g):
        @pl.loop(0, rp)
        def _(i):
            res_copy(g, i).start()

    barrier = pltpu.get_barrier_semaphore()
    me = r * C + c

    @pl.loop(1, R * C)
    def _(k):
        t = lax.rem(me + k, R * C)
        pl.semaphore_signal(
            barrier, inc=1, device_id=(lax.div(t, C), lax.rem(t, C)), device_id_type=MESH
        )

    pl.semaphore_wait(barrier, R * C - 1)

    def panel_sends(act):
        for part in range(2):
            for piece in range(q):
                for tr in range(R):
                    first, count = (0, 1) if part == 0 else (1, K)
                    act(
                        pan.at[pl.ds(first, count), pl.ds(piece * ng, ng)],
                        av.at[pl.ds(first, count)],
                        pan_send.at[part, piece, tr],
                        av_sem.at[part],
                        jnp.int32(tr),
                        r * q + piece,
                    )

    @pl.when(c == 0)
    def _():
        arrived(ring.at[pl.ds(0, q)], pan_sem)

        @pl.loop(0, groups)
        def _(g):
            slot = lax.div(g, ng)
            for s in range(G):
                at = pl.multiple_of((lax.rem(g, ng) * G + s) * LANES, LANES)
                turned = ring[slot, :, pl.ds(at, LANES)].T
                for k in range(K + 1):
                    pan[k, g, s : s + 1, :] = turned[k : k + 1, :]

        panel_sends(send)

    if sp:
        for seq in range(min(nring, K * groups * sp)):
            ring_copy(jnp.int32(seq)).start()

    sub = lax.broadcasted_iota(jnp.int32, (G, LANES), 0)
    lane = lax.broadcasted_iota(jnp.int32, (G, LANES), 1)
    where_at = [c * cols + (n * G + sub) * LANES + lane for n in range(ng)]
    lane1 = lax.broadcasted_iota(jnp.int32, (1, LANES), 1)
    first_col = (jnp.zeros((1, LANES), jnp.int32) + c) == 0

    def load(ref, *at):
        return [ref[(*at, n)] for n in range(ng)]

    def store(ref, value, *at):
        for n in range(ng):
            ref[(*at, n)] = value[n]

    def pick(row, k):
        return lane_total(jnp.where(lane1 == k, row, 0.0))

    def dots(one, two):
        total = one[0] * two[0]
        for n in range(1, ng):
            total = total + one[n] * two[n]
        return jnp.sum(total, axis=0, keepdims=True)

    def less(value, scale, other):
        return [a - scale * b for a, b in zip(value, other)]

    def round_copy(j, k, o):
        tc = lax.rem(c + o, C)
        return pltpu.make_async_remote_copy(
            sbuf.at[j, k], rnd.at[j, k, c], s_send.at[j, k], s_recv.at[j, k],
            device_id=(r, tc), device_id_type=MESH,
        )

    def round_send(j, k):
        rnd[j, k, c] = sbuf[j, k]

        @pl.loop(1, C)
        def _(o):
            round_copy(j, k, o).start()

    def round_get(j, k):
        arrived(rnd.at[j, k, pl.ds(0, C - 1)], s_recv.at[j, k])
        total = rnd[j, k, 0]
        for n in range(1, C):
            total = total + rnd[j, k, n]
        return total

    def p_targets(j, g, act):
        piece, part = lax.div(g, ng), lax.rem(g, ng)
        for tr in range(R):
            act(
                pbuf.at[j, g], rbuf.at[j, c, part], p_send.at[j, g, tr], p_recv.at[j],
                jnp.int32(tr), r * q + piece,
            )

    def o_targets(j, act):
        for u in range(q):
            act(
                vy.at[j], ob.at[j, lax.rem(c, q)], o_send.at[j, u], o_recv.at[j],
                lax.div(c, q), r + R * u,
            )

    diag_sub = lax.broadcasted_iota(jnp.int32, (LANES, LANES), 0)
    diag_lane = lax.broadcasted_iota(jnp.int32, (LANES, LANES), 1)

    def times(chunk, s):
        total = None
        for t in range(m):
            term = chunk[:, t * LANES : (t + 1) * LANES] * xs[t // G, t % G : t % G + 1, :]
            total = term if total is None else total + term
        acc[s] = total

    def multiply_groups(j, low, high):
        @pl.loop(low, high)
        def _(g):
            cuts = [rp * u // max(sp, 1) for u in range(max(sp, 1) + 1)]
            for u in range(max(sp, 1)):
                @pl.loop(cuts[u], cuts[u + 1])
                def _(i):
                    if j == 0:
                        res_copy(g, i).wait()
                    times(res.at[g * rp + i], i)

                if sp:
                    seq = j * groups * sp + g * sp + u
                    ring_copy(seq).wait()
                    times(ring.at[lax.rem(seq, nring)], rp + u)

                    @pl.when(seq + nring < K * groups * sp)
                    def _():
                        ring_copy(seq + nring).start()

            for s in range(G):
                line = jnp.sum(acc[s], axis=1, keepdims=True)
                line = jnp.where(diag_sub == diag_lane, line, 0.0)
                pbuf[j, g, s : s + 1, :] = jnp.sum(line, axis=0, keepdims=True)
            p_targets(j, g, send)

    zero = jnp.zeros((1, 1), jnp.float32)
    v_top, t_cols = [], []
    arrived(av.at[pl.ds(0, 1)], av_sem.at[0])

    for j in range(K):
        x = load(av, j)
        for i in range(j):
            x = less(x, pick(v_top[i], j), load(ys, i))
        store(xs, [jnp.where(w > j + 1, a, 0.0) for w, a in zip(where_at, x)])
        x_top_row = jnp.where(first_col, x[0][0:1, :], 0.0)
        sbuf[j, 0] = jnp.zeros((8, LANES), jnp.float32)
        sbuf[j, 1] = jnp.zeros((8, LANES), jnp.float32)
        sbuf[j, 0 if j else 1, K + 1 : K + 2, :] = x_top_row

        if j:
            for i in range(j):
                sbuf[j, 0, i : i + 1, :] = dots(load(vs, i), x)
            round_send(j, 0)
            multiply_groups(j, 0, groups - 1)
            got = round_get(j, 0)
            left = [lane_total(got[i : i + 1, :]) for i in range(j)]
            w = []
            for k in range(j):
                total = zero
                for i in range(k + 1):
                    total = total + t_cols[k][i] * left[i]
                w.append(total)
            b, b_top = x, got[K + 1 : K + 2, :]
            for i in range(j):
                b = less(b, w[i], load(vs, i))
                b_top = b_top - w[i] * v_top[i]
        else:
            b, w = x, []
        b = [jnp.where(at > j + 1, a, 0.0) for at, a in zip(where_at, b)]
        for i in range(j):
            sbuf[j, 1, i : i + 1, :] = dots(load(vs, i), b)
        sbuf[j, 1, K : K + 1, :] = dots(b, b)
        round_send(j, 1)
        multiply_groups(j, groups - 1 if j else 0, groups)

        got = round_get(j, 1)
        if j == 0:
            b_top = got[K + 1 : K + 2, :]
            arrived(av.at[pl.ds(1, K)], av_sem.at[1])
        squares = lane_total(got[K : K + 1, :])
        pivot = pick(b_top, j + 1)
        length = jnp.sqrt(pivot * pivot + squares)
        beta = -jnp.where(pivot >= 0, 1.0, -1.0) * length
        tau = (beta - pivot) / beta
        div = pivot - beta
        cross = [lane_total(got[i : i + 1, :]) / div + pick(v_top[i], j + 1) for i in range(j)]
        v = [a / div + jnp.where(at == j + 1, 1.0, 0.0) for at, a in zip(where_at, b)]
        store(vs, v, j)
        store(vy, v, j, 1)
        new_top = jnp.where(lane1 > j + 1, b_top / div, 0.0) + jnp.where(lane1 == j + 1, 1.0, 0.0)

        arrived(rbuf.at[j], p_recv.at[j])
        p = load(rbuf, j, 0)
        for n in range(1, C):
            p = [a + b_ for a, b_ in zip(p, load(rbuf, j, n))]
        for i in range(j):
            p = less(p, w[i], load(ps, i))
        for k in range(j + 2):
            if j:
                back = zero
                for i in range(j):
                    back = back - w[i] * pick(v_top[i], k)
                p = less(p, back, load(av, k))
        p = [a / div + e for a, e in zip(p, load(av, j + 1))]
        store(ps, p, j)
        y = p
        for i in range(j):
            y = less(y, cross[i], load(ys, i))
        y = [tau * a for a in y]
        store(ys, y, j)
        store(vy, y, j, 0)
        o_targets(j, send)
        column = []
        for i in range(j):
            total = zero
            for k in range(i, j):
                total = total + t_cols[k][i] * cross[k]
            column.append(-tau * total)
        t_cols.append(column + [tau])
        v_top.append(new_top)

    ti = lax.broadcasted_iota(jnp.int32, (K, K), 0)
    tj = lax.broadcasted_iota(jnp.int32, (K, K), 1)
    t_all = jnp.zeros((K, K), jnp.float32)
    for j in range(K):
        for i in range(j + 1):
            t_all = jnp.where(jnp.logical_and(ti == i, tj == j), t_cols[j][i], t_all)
    t_ref[...] = t_all

    for j in range(K):
        arrived(ob.at[j], o_recv.at[j])
    for h in range(q):
        for n in range(ng):
            for s in range(G):
                at = ((h * ng + n) * G + s) * LANES
                for j in range(K):
                    y_ref[j : j + 1, at : at + LANES] = ob[j, h, 0, n, s : s + 1, :]
                    v_ref[j : j + 1, at : at + LANES] = ob[j, h, 1, n, s : s + 1, :]

    @pl.when(c == 0)
    def _():
        panel_sends(sent)

    for j in range(K):
        for k in range(0 if j else 1, 2):
            arrived(rnd.at[j, k, pl.ds(0, C - 1)], s_send.at[j, k])

        @pl.loop(0, groups)
        def _(g):
            p_targets(j, g, sent)

        o_targets(j, sent)


def solution(mesh):
    R, C = mesh.shape["row"], mesh.shape["col"]

    def on_device(matrix):
        rows, cols = matrix.shape
        q, m, G, ng, groups, ring, sp = plan(R, C, rows, cols)
        f32 = lambda *shape: pltpu.VMEM(shape, jnp.float32)
        dma = lambda *shape: pltpu.SemaphoreType.DMA(shape)
        nres = groups * (G - sp)
        return pl.pallas_call(
            functools.partial(kernel, R, C),
            out_shape=(
                jax.ShapeDtypeStruct((K, rows), jnp.float32),
                jax.ShapeDtypeStruct((K, rows), jnp.float32),
                jax.ShapeDtypeStruct((K, K), jnp.float32),
            ),
            in_specs=[pl.BlockSpec(memory_space=pl.ANY)],
            out_specs=(pl.BlockSpec(memory_space=pltpu.VMEM),) * 3,
            scratch_shapes=[
                f32(nres, LANES, cols),
                f32(ring, LANES, cols),
                f32(G, LANES, LANES),
                f32(K + 1, groups, G, LANES),
                f32(K + 1, ng, G, LANES),
                f32(ng, G, LANES),
                f32(K, groups, G, LANES),
                f32(K, C, ng, G, LANES),
                f32(K, 2, 8, LANES),
                f32(K, 2, C, 8, LANES),
                f32(K, 2, ng, G, LANES),
                f32(K, q, 2, ng, G, LANES),
                f32(K, ng, G, LANES),
                f32(K, ng, G, LANES),
                f32(K, ng, G, LANES),
                dma(nres),
                dma(ring),
                pltpu.SemaphoreType.DMA,
                dma(2, q, R),
                dma(2),
                dma(K, groups, R),
                dma(K),
                dma(K, 2),
                dma(K, 2),
                dma(K, q),
                dma(K),
            ],
            compiler_params=pltpu.CompilerParams(
                collective_id=0, has_side_effects=True, vmem_limit_bytes=VMEM_BYTES
            ),
        )(matrix)

    return jax.shard_map(
        on_device,
        mesh=mesh,
        in_specs=(P("row", "col"),),
        out_specs=(P(None, "row"), P(None, "row"), P()),
        check_vma=False,
    )
```

```python
import functools

import jax
import jax.numpy as jnp
from jax import lax
from jax.experimental import pallas as pl
from jax.experimental.pallas import tpu as pltpu
from jax.sharding import PartitionSpec as P

K = 4
LANES = 128
MESH = pl.DeviceIdType.MESH
VMEM_BYTES = 67043328
SPARE_BYTES = 5 * 2**19


def plan(R, C, rows, cols):
    q = C // R
    m = cols // LANES
    G = 8 if m % 8 == 0 else m
    ng = m // G
    groups = q * ng
    ring = max(4, q)
    room = (VMEM_BYTES - SPARE_BYTES) // (LANES * cols * 4)
    sp = 0
    while (G - sp) * groups + ring > room:
        sp += 1
    return q, m, G, ng, groups, ring, sp


def lane_total(row):
    return jnp.sum(row, axis=-1, keepdims=True)


def kernel(
    R, C, a_hbm, o_ref, t_ref,
    res, ring, acc, pan, av, xs, pbuf, rbuf, sbuf, rnd, vy, ob, vs, ys, ps,
    res_sem, ring_sem, pan_sem, pan_send, av_sem, p_send, p_recv, s_send, s_recv, o_send, o_recv,
):
    rows, cols = a_hbm.shape
    q, m, G, ng, groups, nring, sp = plan(R, C, rows, cols)
    rp = G - sp
    r = lax.axis_index("row")
    c = lax.axis_index("col")

    def send(src, dst, send_sem, recv_sem, tr, tc):
        same = jnp.logical_and(tr == r, tc == c)

        @pl.when(jnp.logical_not(same))
        def _():
            pltpu.make_async_remote_copy(
                src, dst, send_sem, recv_sem, device_id=(tr, tc), device_id_type=MESH
            ).start()

        @pl.when(same)
        def _():
            pltpu.make_async_copy(src, dst, recv_sem).start()

    def sent(src, dst, send_sem, recv_sem, tr, tc):
        same = jnp.logical_and(tr == r, tc == c)

        @pl.when(jnp.logical_not(same))
        def _():
            pltpu.make_async_remote_copy(
                src, dst, send_sem, recv_sem, device_id=(tr, tc), device_id_type=MESH
            ).wait_send()

    def arrived(ref, sem):
        pltpu.make_async_copy(ref, ref, sem).wait()

    def panel_copy(t):
        return pltpu.make_async_copy(
            a_hbm.at[pl.ds(pl.multiple_of(t * LANES, LANES), LANES), pl.ds(0, LANES)],
            ring.at[lax.div(t, m), :, pl.ds(pl.multiple_of(lax.rem(t, m) * LANES, LANES), LANES)],
            pan_sem,
        )

    @pl.when(c == 0)
    def _():
        @pl.loop(0, q * m)
        def _(t):
            panel_copy(t).start()

    def res_copy(g, i):
        row = pl.multiple_of((g * G + i) * LANES, LANES)
        k = g * rp + i
        return pltpu.make_async_copy(a_hbm.at[pl.ds(row, LANES)], res.at[k], res_sem.at[k])

    def ring_copy(seq):
        n = lax.rem(seq, groups * sp)
        g, u = lax.div(n, sp), lax.rem(n, sp)
        row = pl.multiple_of((g * G + rp + u) * LANES, LANES)
        slot = lax.rem(seq, nring)
        return pltpu.make_async_copy(a_hbm.at[pl.ds(row, LANES)], ring.at[slot], ring_sem.at[slot])

    @pl.loop(0, groups)
    def _(g):
        @pl.loop(0, rp)
        def _(i):
            res_copy(g, i).start()

    barrier = pltpu.get_barrier_semaphore()
    me = r * C + c

    @pl.loop(1, R * C)
    def _(k):
        t = lax.rem(me + k, R * C)
        pl.semaphore_signal(
            barrier, inc=1, device_id=(lax.div(t, C), lax.rem(t, C)), device_id_type=MESH
        )

    def panel_sends(act):
        for part in range(2):
            for piece in range(q):
                for tr in range(R):
                    first, count = (0, 1) if part == 0 else (1, K)
                    act(
                        pan.at[pl.ds(first, count), pl.ds(piece * ng, ng)],
                        av.at[pl.ds(first, count)],
                        pan_send.at[part, piece, tr],
                        av_sem.at[part],
                        jnp.int32(tr),
                        r * q + piece,
                    )

    @pl.when(c == 0)
    def _():
        arrived(ring.at[pl.ds(0, q)], pan_sem)

        @pl.loop(0, groups)
        def _(g):
            slot = lax.div(g, ng)
            for s in range(G):
                at = pl.multiple_of((lax.rem(g, ng) * G + s) * LANES, LANES)
                turned = ring[slot, :, pl.ds(at, LANES)].T
                for k in range(K + 1):
                    pan[k, g, s : s + 1, :] = turned[k : k + 1, :]

    pl.semaphore_wait(barrier, R * C - 1)

    @pl.when(c == 0)
    def _():
        panel_sends(send)

    if sp:
        for seq in range(min(nring, K * groups * sp)):
            ring_copy(jnp.int32(seq)).start()

    sub = lax.broadcasted_iota(jnp.int32, (G, LANES), 0)
    lane = lax.broadcasted_iota(jnp.int32, (G, LANES), 1)
    where_at = [c * cols + (n * G + sub) * LANES + lane for n in range(ng)]
    lane1 = lax.broadcasted_iota(jnp.int32, (1, LANES), 1)
    first_col = (jnp.zeros((1, LANES), jnp.int32) + c) == 0

    def load(ref, *at):
        return [ref[(*at, n)] for n in range(ng)]

    def store(ref, value, *at):
        for n in range(ng):
            ref[(*at, n)] = value[n]

    def pick(row, k):
        return lane_total(jnp.where(lane1 == k, row, 0.0))

    def dots(one, two):
        total = one[0] * two[0]
        for n in range(1, ng):
            total = total + one[n] * two[n]
        return jnp.sum(total, axis=0, keepdims=True)

    def less(value, scale, other):
        return [a - scale * b for a, b in zip(value, other)]

    def round_copy(j, k, o):
        tc = lax.rem(c + o, C)
        return pltpu.make_async_remote_copy(
            sbuf.at[j, k], rnd.at[j, k, c], s_send.at[j, k], s_recv.at[j, k],
            device_id=(r, tc), device_id_type=MESH,
        )

    def round_send(j, k):
        rnd[j, k, c] = sbuf[j, k]

        @pl.loop(1, C)
        def _(o):
            round_copy(j, k, o).start()

    def round_get(j, k):
        arrived(rnd.at[j, k, pl.ds(0, C - 1)], s_recv.at[j, k])
        total = rnd[j, k, 0]
        for n in range(1, C):
            total = total + rnd[j, k, n]
        return total

    def p_targets(j, g, act):
        piece, part = lax.div(g, ng), lax.rem(g, ng)
        for tr in range(R):
            act(
                pbuf.at[j, g], rbuf.at[j, c, part], p_send.at[j, g, tr], p_recv.at[j],
                jnp.int32(tr), r * q + piece,
            )

    def o_targets(j, act):
        for u in range(q):
            act(
                vy.at[j], ob.at[j, lax.rem(c, q)], o_send.at[j, u], o_recv.at[j],
                lax.div(c, q), r + R * u,
            )

    diag_sub = lax.broadcasted_iota(jnp.int32, (LANES, LANES), 0)
    diag_lane = lax.broadcasted_iota(jnp.int32, (LANES, LANES), 1)

    def times(chunk, s):
        total = None
        for t in range(m):
            term = chunk[:, t * LANES : (t + 1) * LANES] * xs[t // G, t % G : t % G + 1, :]
            total = term if total is None else total + term
        acc[s] = total

    def multiply_groups(j, low, high):
        @pl.loop(low, high)
        def _(g):
            cuts = [rp * u // max(sp, 1) for u in range(max(sp, 1) + 1)]
            for u in range(max(sp, 1)):
                @pl.loop(cuts[u], cuts[u + 1])
                def _(i):
                    if j == 0:
                        res_copy(g, i).wait()
                    times(res.at[g * rp + i], i)

                if sp:
                    seq = j * groups * sp + g * sp + u
                    ring_copy(seq).wait()
                    times(ring.at[lax.rem(seq, nring)], rp + u)

                    @pl.when(seq + nring < K * groups * sp)
                    def _():
                        ring_copy(seq + nring).start()

            for s in range(G):
                line = jnp.sum(acc[s], axis=1, keepdims=True)
                line = jnp.where(diag_sub == diag_lane, line, 0.0)
                pbuf[j, g, s : s + 1, :] = jnp.sum(line, axis=0, keepdims=True)
            p_targets(j, g, send)

    zero = jnp.zeros((1, 1), jnp.float32)
    early = groups - max(1, groups // 3)
    v_top, t_cols = [], []
    arrived(av.at[pl.ds(0, 1)], av_sem.at[0])

    for j in range(K):
        if j == 0:
            x = load(av, 0)
        store(xs, [jnp.where(w > j + 1, a, 0.0) for w, a in zip(where_at, x)])
        x_top_row = jnp.where(first_col, x[0][0:1, :], 0.0)
        sbuf[j, 0] = jnp.zeros((8, LANES), jnp.float32)
        sbuf[j, 1] = jnp.zeros((8, LANES), jnp.float32)
        sbuf[j, 0 if j else 1, K + 1 : K + 2, :] = x_top_row

        if j:
            for i in range(j):
                sbuf[j, 0, i : i + 1, :] = dots(load(vs, i), x)
            round_send(j, 0)
            o_targets(j - 1, send)
            multiply_groups(j, 0, early)
            got = round_get(j, 0)
            left = [lane_total(got[i : i + 1, :]) for i in range(j)]
            w = []
            for k in range(j):
                total = zero
                for i in range(k + 1):
                    total = total + t_cols[k][i] * left[i]
                w.append(total)
            b, b_top = x, got[K + 1 : K + 2, :]
            for i in range(j):
                b = less(b, w[i], load(vs, i))
                b_top = b_top - w[i] * v_top[i]
        else:
            b, w = x, []
        b = [jnp.where(at > j + 1, a, 0.0) for at, a in zip(where_at, b)]
        for i in range(j):
            sbuf[j, 1, i : i + 1, :] = dots(load(vs, i), b)
        sbuf[j, 1, K : K + 1, :] = dots(b, b)
        round_send(j, 1)
        multiply_groups(j, early if j else 0, groups)

        got = round_get(j, 1)
        if j == 0:
            b_top = got[K + 1 : K + 2, :]
            arrived(av.at[pl.ds(1, K)], av_sem.at[1])
        squares = lane_total(got[K : K + 1, :])
        pivot = pick(b_top, j + 1)
        length = jnp.sqrt(pivot * pivot + squares)
        beta = -jnp.where(pivot >= 0, 1.0, -1.0) * length
        tau = (beta - pivot) / beta
        div = pivot - beta
        cross = [lane_total(got[i : i + 1, :]) / div + pick(v_top[i], j + 1) for i in range(j)]
        v = [a / div + jnp.where(at == j + 1, 1.0, 0.0) for at, a in zip(where_at, b)]
        store(vs, v, j)
        store(vy, v, j, 1)
        new_top = jnp.where(lane1 > j + 1, b_top / div, 0.0) + jnp.where(lane1 == j + 1, 1.0, 0.0)

        v_top.append(new_top)
        column = []
        for i in range(j):
            total = zero
            for k in range(i, j):
                total = total + t_cols[k][i] * cross[k]
            column.append(-tau * total)
        t_cols.append(column + [tau])

        fix = [jnp.zeros((G, LANES), jnp.float32)] * ng
        for i in range(j):
            fix = less(fix, w[i], load(ps, i))
        for k in range(j + 2 if j else 0):
            back = zero
            for i in range(j):
                back = back - w[i] * pick(v_top[i], k)
            fix = less(fix, back, load(av, k))
        y_fix = load(av, j + 1)
        for i in range(j):
            y_fix = less(y_fix, cross[i], load(ys, i))
        if j + 1 < K:
            x = load(av, j + 1)
            for i in range(j):
                x = less(x, pick(v_top[i], j + 1), load(ys, i))
            entry = pick(new_top, j + 1)

        arrived(rbuf.at[j], p_recv.at[j])
        p = load(rbuf, j, 0)
        for n in range(1, C):
            p = [a + b_ for a, b_ in zip(p, load(rbuf, j, n))]
        p = [(a + e) / div for a, e in zip(p, fix)]
        y = [tau * (a + e) for a, e in zip(p, y_fix)]
        if j + 1 < K:
            x = less(x, entry, y)
        store(vy, y, j, 0)
        store(ys, y, j)
        store(ps, [a + e for a, e in zip(p, load(av, j + 1))], j)
        if j + 1 == K:
            o_targets(j, send)

    ti = lax.broadcasted_iota(jnp.int32, (K, K), 0)
    tj = lax.broadcasted_iota(jnp.int32, (K, K), 1)
    t_all = jnp.zeros((K, K), jnp.float32)
    for j in range(K):
        for i in range(j + 1):
            t_all = jnp.where(jnp.logical_and(ti == i, tj == j), t_cols[j][i], t_all)
    t_ref[...] = t_all

    for j in range(K):
        arrived(ob.at[j], o_recv.at[j])
    o_ref[...] = ob[...]

    @pl.when(c == 0)
    def _():
        panel_sends(sent)

    for j in range(K):
        for k in range(0 if j else 1, 2):
            arrived(rnd.at[j, k, pl.ds(0, C - 1)], s_send.at[j, k])

        @pl.loop(0, groups)
        def _(g):
            p_targets(j, g, sent)

        o_targets(j, sent)


def lay_out(o_ref, t_in, y_ref, v_ref, t_ref):
    _, q, _, ng, G, _ = o_ref.shape
    for h in range(q):
        for n in range(ng):
            for s in range(G):
                at = ((h * ng + n) * G + s) * LANES
                for j in range(K):
                    y_ref[j : j + 1, at : at + LANES] = o_ref[j, h, 0, n, s : s + 1, :]
                    v_ref[j : j + 1, at : at + LANES] = o_ref[j, h, 1, n, s : s + 1, :]
    t_ref[...] = t_in[...]


def solution(mesh):
    R, C = mesh.shape["row"], mesh.shape["col"]

    def on_device(matrix):
        rows, cols = matrix.shape
        q, m, G, ng, groups, ring, sp = plan(R, C, rows, cols)
        f32 = lambda *shape: pltpu.VMEM(shape, jnp.float32)
        dma = lambda *shape: pltpu.SemaphoreType.DMA(shape)
        nres = groups * (G - sp)
        blocks, t_block = pl.pallas_call(
            functools.partial(kernel, R, C),
            out_shape=(
                jax.ShapeDtypeStruct((K, q, 2, ng, G, LANES), jnp.float32),
                jax.ShapeDtypeStruct((K, K), jnp.float32),
            ),
            in_specs=[pl.BlockSpec(memory_space=pl.ANY)],
            out_specs=(pl.BlockSpec(memory_space=pltpu.VMEM),) * 2,
            scratch_shapes=[
                f32(nres, LANES, cols),
                f32(ring, LANES, cols),
                f32(G, LANES, LANES),
                f32(K + 1, groups, G, LANES),
                f32(K + 1, ng, G, LANES),
                f32(ng, G, LANES),
                f32(K, groups, G, LANES),
                f32(K, C, ng, G, LANES),
                f32(K, 2, 8, LANES),
                f32(K, 2, C, 8, LANES),
                f32(K, 2, ng, G, LANES),
                f32(K, q, 2, ng, G, LANES),
                f32(K, ng, G, LANES),
                f32(K, ng, G, LANES),
                f32(K, ng, G, LANES),
                dma(nres),
                dma(ring),
                pltpu.SemaphoreType.DMA,
                dma(2, q, R),
                dma(2),
                dma(K, groups, R),
                dma(K),
                dma(K, 2),
                dma(K, 2),
                dma(K, q),
                dma(K),
            ],
            compiler_params=pltpu.CompilerParams(
                collective_id=0, has_side_effects=True, vmem_limit_bytes=VMEM_BYTES
            ),
        )(matrix)
        return pl.pallas_call(
            lay_out,
            out_shape=(
                jax.ShapeDtypeStruct((K, rows), jnp.float32),
                jax.ShapeDtypeStruct((K, rows), jnp.float32),
                jax.ShapeDtypeStruct((K, K), jnp.float32),
            ),
            in_specs=[pl.BlockSpec(memory_space=pltpu.VMEM)] * 2,
            out_specs=(pl.BlockSpec(memory_space=pltpu.VMEM),) * 3,
        )(blocks, t_block)

    return jax.shard_map(
        on_device,
        mesh=mesh,
        in_specs=(P("row", "col"),),
        out_specs=(P(None, "row"), P(None, "row"), P()),
        check_vma=False,
    )
```
